256 devices in a mesh: mem: 16 (over z, x_lo), lon: 16 (over x_hi, y, core).
Axes of the slice: x: 4 (x_hi: 2, x_lo: 2; x = x_hi * 2 + x_lo), y: 4, z: 8, core: 2. Of those that a mesh axis runs over, the one named last changes fastest.
Arguments:
- state: bfloat16 [256, 65536], P('mem', 'lon'), may hold values from -6 to 6
- hx: bfloat16 [512, 256, 128], P('lon'), may hold values from -6 to 6
- obs_value: float32 [512, 128], P('lon'), may hold values from -10 to 10
- obs_rinv: float32 [512, 128], P('lon'), may hold values from 0.3 to 3
- obs_count: int32 [512], P('lon'), may hold values from 1 to 128
- loc_pattern: int32 [512, 8], P('lon'), may hold values from 0 to 95, as said below
Outputs:
- analysis: bfloat16 [256, 65536], P('mem', 'lon')
The draws below stay inside these ranges and needn't reach their ends.
Inputs may be any that keep to these rules, and one draw needn't show every extreme that they name: obs_count[n] is how many of block n's first observations are valid; the rest are ignored. Each row of loc_pattern holds 8 different window positions out of 96: the previous region's blocks, the patch's own region's blocks, the next region's blocks, around the closed longitude loop.
All inputs are finite; a program needn't handle non-finite values.
Results may differ from the reference program's by a relative error of at most 0.0065.
Values may be sent and summed in bfloat16 or wider, within the bound.
A program may use at most 64 MiB of HBM per device.

```python
import math
import jax
import jax.numpy as jnp
from jax import lax

K = 256
B = 128
PTS = 128
BLK_DEV = 32
USE = 8
ITERS = 6
RP = 32
NPATCH = 512
G = 65536
NBLK = 512


def draw_loc_pattern(key, part):
    window = 3 * BLK_DEV
    scores = jax.random.randint(key, (NPATCH, window), 0, 1 << 20) * window + jnp.arange(window, dtype=jnp.int32)[None, :]
    chosen = lax.top_k(scores, USE)[1]
    return chosen.astype(jnp.int32)


def plant(values, rng, least, high):
    dims = values.shape
    place = [jax.random.randint(jax.random.fold_in(rng, axis), (), 0, dims[axis]) for axis in range(len(dims))]
    values = values.at[tuple(place)].set(least)
    longest = dims.index(max(dims))
    place[longest] = (place[longest] + 1) % dims[longest]
    return values.at[tuple(place)].set(high)


def levels(own_key, extent, shards, smallest, top_value):
    factor_of = 1.0
    for dim, parts in shards:
        draws = jax.random.uniform(jax.random.fold_in(jax.random.fold_in(own_key, 6), dim), (parts,), jnp.float32, smallest / len(shards), top_value / len(shards))
        factor_of = factor_of * jnp.repeat(jnp.exp(draws), extent[dim] // parts).reshape((-1,) + (1,) * (len(extent) - 1 - dim))
    return factor_of


def centred(stream_key, extent, width, bound, split=(), kind=jnp.bfloat16):
    drawn = width * jax.random.normal(stream_key, extent, jnp.float32)
    if split:
        drawn = drawn * levels(stream_key, extent, split, -0.22, 0.18)
    return jnp.clip(drawn, -bound, bound).astype(kind)


def setup_inputs(seed: int = 0) -> dict:
    key_list = jax.random.split(jax.random.key(seed), 7)
    state = centred(key_list[0], (K, G), 1.0, 6.0, ((0, 16), (1, 16)))
    hx = centred(key_list[1], (NBLK, K, B), 1.0, 6.0, ((0, 16),))
    obs_value = centred(key_list[2], (NBLK, B), 2.0, 10.0, ((0, 16),), jnp.float32)
    obs_rinv = jnp.clip(jnp.exp(math.log(3.0) - 2.3025851 * jax.random.uniform(key_list[3], (NBLK, B), jnp.float32) ** levels(key_list[3], (NBLK, B), ((0, 16),), -0.2, 0.2)), 0.3, 3.0)
    obs_count = plant(jax.random.randint(key_list[4], (NBLK,), 1, B + 1), jax.random.fold_in(key_list[4], 1), 1, B).astype(jnp.int32)
    loc_pattern = draw_loc_pattern(jax.random.fold_in(key_list[6], 71), 0)
    return dict(state=state, hx=hx, obs_value=obs_value, obs_rinv=obs_rinv, obs_count=obs_count, loc_pattern=loc_pattern)


def reference(state, hx, obs_value, obs_rinv, obs_count, loc_pattern):
    high = lax.Precision.HIGHEST
    obs_mean = lax.optimization_barrier(jnp.sum(hx.astype(jnp.float32), axis=1)) / K
    obs_pert = (hx.astype(jnp.float32) - obs_mean[:, None, :]).astype(jnp.bfloat16)
    valid = jnp.arange(B, dtype=jnp.int32)[None, :] < obs_count[:, None]
    weight = jnp.where(valid, obs_rinv, jnp.float32(0.0))
    innov = weight * (obs_value - obs_mean)
    weight_b = weight.astype(jnp.bfloat16)
    innov_b = innov.astype(jnp.bfloat16)
    scaled = (weight_b.astype(jnp.float32)[:, None, :] * obs_pert.astype(jnp.float32)).astype(jnp.bfloat16)
    eye = jnp.eye(K, dtype=jnp.float32)

    def one_patch(patch):
        region = patch // RP
        rank = patch % RP
        picks = loc_pattern[patch]
        blocks = (region * BLK_DEV - BLK_DEV + picks) % NBLK
        offset = (picks.astype(jnp.float32) + 0.5) / BLK_DEV - 1.0 - (rank.astype(jnp.float32) + 0.5) / RP
        taper = jnp.exp(-0.5 * offset * offset)
        system = (K - 1.0) * eye
        forcing = jnp.zeros((K,), jnp.float32)
        for slot in range(USE):
            block = blocks[slot]
            gram = jnp.dot(obs_pert[block], scaled[block].T, preferred_element_type=jnp.float32)
            vec = jnp.dot(obs_pert[block], innov_b[block], preferred_element_type=jnp.float32)
            system = system + taper[slot] * gram
            forcing = forcing + taper[slot] * vec
        scale = jnp.sqrt(jnp.sum(system * system))
        iterate = system / scale
        root = eye
        for step in range(ITERS):
            factor = 1.5 * eye - 0.5 * jnp.dot(root, iterate, precision=high)
            iterate = jnp.dot(iterate, factor, precision=high)
            root = jnp.dot(factor, root, precision=high)
        root = root / jnp.sqrt(scale)
        mean_weight = jnp.dot(root, jnp.dot(root, forcing, precision=high), precision=high)
        transform = jnp.sqrt(jnp.float32(K - 1.0)) * root + mean_weight[:, None]
        columns = lax.dynamic_slice(state, (jnp.int32(0), (patch * PTS).astype(jnp.int32)), (K, PTS))
        state_mean = lax.optimization_barrier(jnp.sum(columns.astype(jnp.float32), axis=0)) / K
        deviation = columns.astype(jnp.float32) - state_mean[None, :]
        updated = state_mean[None, :] + jnp.dot(transform.T, deviation, precision=high)
        return updated.astype(jnp.bfloat16)
    result = lax.map(one_patch, jnp.arange(NPATCH, dtype=jnp.int32))
    return jnp.transpose(result, (1, 0, 2)).reshape(K, NPATCH * PTS)
```

```python
import functools

import jax
import jax.numpy as jnp
from jax import lax
from jax.experimental import pallas as pl
from jax.experimental.pallas import tpu as pltpu
from jax.sharding import PartitionSpec as P

MESH = pl.DeviceIdType.MESH
F32, BF16 = jnp.float32, jnp.bfloat16
USE = 8
PAT = 2
EXTRA = 16
CHUNKS = 4
E_STEPS = 3


def dot(a, b):
    return lax.dot_general(a, b, (((1,), (0,)), ((), ())), preferred_element_type=F32)


def dot_nt(a, b):
    return lax.dot_general(a, b, (((1,), (1,)), ((), ())), preferred_element_type=F32)


def kernel(
    n_mem, n_lon,
    state_ref, hx_ref, value_ref, rinv_ref, count_ref, loc_ref,
    out_ref,
    pert, weight, innov, lhs, rhs, own, send, recv, gathered, rows, answer, loc_far,
    hx_sem, here_sem, loc_send, loc_recv, part_send, part_recv, in_send, in_recv, ans_send, ans_recv,
):
    mem, lon = lax.axis_index("mem"), lax.axis_index("lon")
    blocks, members, width = hx_ref.shape
    local = state_ref.shape[0]
    cols = state_ref.shape[1] // n_mem
    pts = cols // PAT
    ranks = n_mem * PAT

    odd = lon % 2
    sign = 2 * odd - 1
    wrap = (lon + odd) % 8 == 0
    crossed = mem + 1 - 2 * (mem % 2)
    partners = (
        ((lon + sign + n_lon) % n_lon, jnp.where(wrap, crossed, mem), sign),
        ((lon - sign + n_lon) % n_lon, mem, -sign),
    )

    per = blocks // CHUNKS
    fetches = []
    for c in range(CHUNKS):
        part = pl.ds(c * per, per)
        fetch = pltpu.make_async_copy(hx_ref.at[part], pert.at[part], hx_sem.at[c])
        fetch.start()
        fetches.append(fetch)
    mine_rows = pl.ds(pl.multiple_of(mem * local, local), local)
    mine_cols = pl.ds(pl.multiple_of(mem * cols, cols), cols)
    keep = pltpu.make_async_copy(state_ref.at[:, mine_cols], gathered.at[mine_rows, :], here_sem.at[0])
    keep.start()

    barrier = pltpu.get_barrier_semaphore()
    for p_lon, p_mem, _ in partners:
        pl.semaphore_signal(barrier, inc=1, device_id=(p_mem, p_lon), device_id_type=MESH)
    peers = [(mem + d) % n_mem for d in range(1, n_mem)]
    for peer in peers:
        pl.semaphore_signal(barrier, inc=1, device_id=(peer, lon), device_id_type=MESH)

    lane = lax.broadcasted_iota(jnp.int32, (1, width), 1)

    def prepare(b):
        x = pert[b].astype(F32)
        mean = jnp.sum(x, axis=0, keepdims=True) * (1.0 / members)
        pert[b] = (x - mean).astype(BF16)
        w = jnp.where(lane < count_ref[b], rinv_ref[pl.ds(b, 1), :], 0.0)
        weight[pl.ds(b, 1), :] = w.astype(BF16).astype(F32)
        innov[pl.ds(b, 1), :] = (w * (value_ref[pl.ds(b, 1), :] - mean)).astype(BF16).astype(F32)

    for c in range(CHUNKS):
        fetches[c].wait()

        @pl.loop(0, per // 4)
        def _(g):
            for k in range(4):
                prepare(c * per + g * 4 + k)

    pl.semaphore_wait(barrier, n_mem + 1)

    loc_moves = []
    for q, (p_lon, p_mem, _) in enumerate(partners):
        move = pltpu.make_async_remote_copy(
            src_ref=loc_ref, dst_ref=loc_far.at[q],
            send_sem=loc_send.at[q], recv_sem=loc_recv.at[q],
            device_id=(p_mem, p_lon), device_id_type=MESH,
        )
        move.start()
        loc_moves.append(move)
    state_moves = []
    for d, peer in enumerate(peers):
        theirs = pl.ds(pl.multiple_of(peer * cols, cols), cols)
        move = pltpu.make_async_remote_copy(
            src_ref=state_ref.at[:, theirs], dst_ref=gathered.at[mine_rows, :],
            send_sem=in_send.at[d], recv_sem=in_recv.at[d],
            device_id=(peer, lon), device_id_type=MESH,
        )
        move.start()
        state_moves.append(move)

    sub = lax.broadcasted_iota(jnp.int32, (EXTRA, width), 0)

    def partial(picks, base, rank):
        for s in range(USE):
            u = picks(s)
            rel = u - base
            inside = jnp.logical_and(rel >= 0, rel < blocks)
            b = jnp.clip(rel, 0, blocks - 1)
            uf = jnp.full((1, width), u, jnp.int32).astype(F32)
            rf = jnp.full((1, width), rank, jnp.int32).astype(F32)
            t = (uf + 0.5) / blocks - 1.0 - (rf + 0.5) / ranks
            taper = jnp.exp(-0.5 * t * t) * jnp.full((1, width), inside.astype(jnp.int32), jnp.int32).astype(F32)
            block = pert[b]
            w = jnp.broadcast_to(weight[pl.ds(b, 1), :] * taper, (EXTRA, width)).astype(BF16)
            scaled = (block.reshape(members // EXTRA, EXTRA, width) * w[None]).reshape(members, width)
            v = jnp.broadcast_to(innov[pl.ds(b, 1), :] * taper, (EXTRA, width))
            high = v.astype(BF16).astype(F32)
            tail = jnp.where(sub == 0, high, jnp.where(sub == 1, v - high, 0.0)).astype(BF16)
            at = pl.ds(s * width, width)
            lhs[pl.ds(0, members), at] = scaled
            lhs[pl.ds(members, EXTRA), at] = tail
            rhs[:, at] = block
        return dot_nt(lhs[...], rhs[...])

    for j in range(PAT):
        rank = mem * PAT + j
        own[j] = partial(lambda s: loc_ref[rank, s], blocks, rank)

    row_id = lax.broadcasted_iota(jnp.int32, (EXTRA, members), 0)
    part_moves = []
    for q, (p_lon, p_mem, s_q) in enumerate(partners):
        loc_moves[q].wait_recv()
        for j in range(PAT):
            rank = p_mem * PAT + j
            got = partial(lambda s: loc_far[q, rank, s], blocks - blocks * s_q, rank)
            send[q, j, pl.ds(0, members), :] = got[:members].astype(BF16)
            force = got[members : members + 1] + got[members + 1 : members + 2]
            high = force.astype(BF16).astype(F32)
            both = jnp.where(row_id == 0, high, jnp.where(row_id == 1, force - high, 0.0))
            send[q, j, pl.ds(members, EXTRA), :] = both.astype(BF16)
            move = pltpu.make_async_remote_copy(
                src_ref=send.at[q, j], dst_ref=recv.at[q, j],
                send_sem=part_send.at[q, j], recv_sem=part_recv.at[q, j],
                device_id=(p_mem, p_lon), device_id_type=MESH,
            )
            move.start()
            part_moves.append(move)

    keep.wait()
    for move in state_moves:
        move.wait_recv()
    g = gathered[...].astype(F32)
    state_mean = jnp.sum(g, axis=0, keepdims=True) * (1.0 / members)
    rows[...] = (g - state_mean).T

    diag = lax.broadcasted_iota(jnp.int32, (members, members), 0) == lax.broadcasted_iota(
        jnp.int32, (members, members), 1
    )
    for move in part_moves:
        move.wait_recv()

    mats, carried, scales = [], [], []
    for j in range(PAT):
        a = own[j, pl.ds(0, members), :]
        force = own[j, pl.ds(members, 1), :] + own[j, pl.ds(members + 1, 1), :]
        for q in range(2):
            a = a + recv[q, j, pl.ds(0, members), :].astype(F32)
            f = recv[q, j, pl.ds(members, EXTRA), :].astype(F32)
            force = force + f[0:1] + f[1:2]
        a = a + jnp.where(diag, members - 1.0, 0.0)
        norm2 = jnp.sum(jnp.sum(a * a, axis=0, keepdims=True), axis=1, keepdims=True)
        inv = lax.rsqrt(norm2)
        mats.append(a * inv)
        scales.append(jnp.sqrt(inv))
        pad = jnp.where(row_id[:8] == 0, jnp.broadcast_to(force, (8, members)), 0.0)
        carried.append(jnp.concatenate([rows[pl.ds(j * pts, pts), :], pad], axis=0))

    for step in range(6):
        for j in range(PAT):
            e = mats[j]
            eb = e.astype(BF16)
            moved = dot(carried[j].astype(BF16), eb)
            if step < E_STEPS:
                carried[j] = 1.5 * carried[j] - 0.5 * moved
            else:
                carried[j] = carried[j] + 0.5 * moved
            if step < 5:
                square = dot(eb, eb)
                cube = dot(square.astype(BF16), eb)
                if step < E_STEPS:
                    e = 2.25 * e - 1.5 * square + 0.25 * cube
                    if step == E_STEPS - 1:
                        e = jnp.where(diag, 1.0, 0.0) - e
                else:
                    e = 0.75 * square + 0.25 * cube
                mats[j] = e

    for j in range(PAT):
        x = carried[j] * scales[j]
        d, u = x[:pts], x[pts : pts + 1]
        shift = jnp.sum(d * u, axis=1, keepdims=True)
        y = (jnp.sqrt(jnp.float32(members - 1.0)) * d + shift).T
        at = pl.ds(j * pts, pts)
        answer[:, at] = (y + state_mean[:, j * pts : (j + 1) * pts]).astype(BF16)

    stay = pltpu.make_async_copy(answer.at[mine_rows, :], out_ref.at[:, mine_cols], here_sem.at[1])
    stay.start()
    ans_moves = []
    for d, peer in enumerate(peers):
        theirs = pl.ds(pl.multiple_of(peer * local, local), local)
        move = pltpu.make_async_remote_copy(
            src_ref=answer.at[theirs, :], dst_ref=out_ref.at[:, mine_cols],
            send_sem=ans_send.at[d], recv_sem=ans_recv.at[d],
            device_id=(peer, lon), device_id_type=MESH,
        )
        move.start()
        ans_moves.append(move)
    for move in loc_moves + state_moves + part_moves:
        move.wait_send()
    stay.wait()
    for move in ans_moves:
        move.wait()


def solution(mesh):
    n_mem, n_lon = mesh.shape["mem"], mesh.shape["lon"]

    def body(state, hx, obs_value, obs_rinv, obs_count, loc_pattern):
        blocks, members, width = hx.shape
        local, points = state.shape
        cols = points // n_mem
        peers = n_mem - 1
        high = members + EXTRA
        dma = pltpu.SemaphoreType.DMA
        any_, vmem, smem = (pl.BlockSpec(memory_space=s) for s in (pl.ANY, pltpu.VMEM, pltpu.SMEM))
        return pl.pallas_call(
            functools.partial(kernel, n_mem, n_lon),
            out_shape=jax.ShapeDtypeStruct((local, points), BF16),
            in_specs=[any_, any_, vmem, vmem, smem, smem],
            out_specs=OUT_SPEC,
            scratch_shapes=[
                pltpu.VMEM((blocks, members, width), BF16),
                pltpu.VMEM((blocks, width), F32),
                pltpu.VMEM((blocks, width), F32),
                pltpu.VMEM((high, USE * width), BF16),
                pltpu.VMEM((members, USE * width), BF16),
                pltpu.VMEM((PAT, high, members), F32),
                pltpu.VMEM((2, PAT, high, members), BF16),
                pltpu.VMEM((2, PAT, high, members), BF16),
                pltpu.VMEM((members, cols), BF16),
                pltpu.VMEM((cols, members), F32),
                pltpu.VMEM((members, cols), BF16),
                pltpu.SMEM((2,) + loc_pattern.shape, jnp.int32),
                dma((CHUNKS,)),
                dma((2,)),
                dma((2,)),
                dma((2,)),
                dma((2, PAT)),
                dma((2, PAT)),
                dma((peers,)),
                dma((peers,)),
                dma((peers,)),
                dma((peers,)),
            ],
            compiler_params=pltpu.CompilerParams(collective_id=0, has_side_effects=True, vmem_limit_bytes=48 << 20),
        )(state, hx, obs_value, obs_rinv, obs_count, loc_pattern)

    in_specs = (
        P("mem", "lon"),
        P("lon", None, None),
        P("lon", None),
        P("lon", None),
        P("lon"),
        P("lon", None),
    )
    return jax.shard_map(body, mesh=mesh, in_specs=in_specs, out_specs=P("mem", "lon"), check_vma=False)


OUT_SPEC = pl.BlockSpec(memory_space=pltpu.VMEM)
```

```python
import functools

import jax
import jax.numpy as jnp
from jax import lax
from jax.experimental import pallas as pl
from jax.experimental.pallas import tpu as pltpu
from jax.sharding import PartitionSpec as P

MESH = pl.DeviceIdType.MESH
F32, BF16 = jnp.float32, jnp.bfloat16
USE = 8
PAT = 2
TAIL = 16
CHUNKS = 4
ITERS = 6
E_STEPS = 3


def dot(a, b):
    return lax.dot_general(a, b, (((1,), (0,)), ((), ())), preferred_element_type=F32)


def dot_nt(a, b):
    return lax.dot_general(a, b, (((1,), (1,)), ((), ())), preferred_element_type=F32)


def halves(x):
    high = x.astype(BF16).astype(F32)
    return high, x - high


def kernel(
    n_mem, n_lon,
    state_ref, hx_ref, value_hbm, rinv_hbm, count_hbm, loc_hbm,
    out_ref,
    pert, value_ref, rinv_ref, count_ref, loc_ref, weight, innov, lhs, rhs, own, own_tail, send, recv, gathered, answer, loc_far,
    hx_sem, small_sem, here_sem, loc_send, loc_recv, part_send, part_recv, in_send, in_recv, ans_send, ans_recv,
    near_sem, far_sem, side_sem,
):
    mem, lon = lax.axis_index("mem"), lax.axis_index("lon")
    blocks, members, width = hx_ref.shape
    half = members // 2
    local = state_ref.shape[0]
    cols = state_ref.shape[1] // n_mem
    pts = cols // PAT
    ranks = n_mem * PAT
    n_z = n_mem // 2
    z, x = mem // 2, mem % 2

    odd = lon % 2
    sign = 2 * odd - 1
    wrap = (lon + odd) % 8 == 0
    crossed = mem + 1 - 2 * x
    partners = (
        ((lon + sign + n_lon) % n_lon, jnp.where(wrap, crossed, mem), sign),
        ((lon - sign + n_lon) % n_lon, mem, -sign),
    )

    def along(step):
        return ((z + step + n_z) % n_z) * 2 + x

    def signal(sem, to_mem, to_lon):
        pl.semaphore_signal(sem, inc=1, device_id=(to_mem, to_lon), device_id_type=MESH)

    barrier = pltpu.get_barrier_semaphore()
    for p_lon, p_mem, _ in partners:
        signal(barrier, p_mem, p_lon)
    for step in (1, -1):
        signal(barrier, along(step), lon)
    signal(barrier, crossed, lon)

    smalls = []
    for i, (src, dst) in enumerate(
        ((loc_hbm, loc_ref), (count_hbm, count_ref), (rinv_hbm, rinv_ref), (value_hbm, value_ref))
    ):
        move = pltpu.make_async_copy(src, dst, small_sem.at[i])
        move.start()
        smalls.append(move)
    per = blocks // CHUNKS
    fetches = []
    for c in range(CHUNKS):
        part = pl.ds(c * per, per)
        fetch = pltpu.make_async_copy(hx_ref.at[part], pert.at[part], hx_sem.at[c])
        fetch.start()
        fetches.append(fetch)
    mine_rows = pl.ds(pl.multiple_of(mem * local, local), local)
    mine_cols = pl.ds(pl.multiple_of(mem * cols, cols), cols)
    keep = pltpu.make_async_copy(state_ref.at[:, mine_cols], gathered.at[mine_rows, :], here_sem.at[0])
    keep.start()
    for move in smalls:
        move.wait()

    lane = lax.broadcasted_iota(jnp.int32, (1, width), 1)

    def prepare(b):
        v = pert[b].astype(F32)
        mean = jnp.sum(v, axis=0, keepdims=True) * (1.0 / members)
        pert[b] = (v - mean).astype(BF16)
        w = jnp.where(lane < count_ref[b], rinv_ref[pl.ds(b, 1), :], 0.0)
        weight[pl.ds(b, 1), :] = w.astype(BF16).astype(F32)
        innov[pl.ds(b, 1), :] = (w * (value_ref[pl.ds(b, 1), :] - mean)).astype(BF16).astype(F32)

    def prepare_chunk(c):
        fetches[c].wait()

        @pl.loop(0, per // 4)
        def _(g):
            for k in range(4):
                prepare(c * per + g * 4 + k)

    for c in range(CHUNKS // 2):
        prepare_chunk(c)

    pl.semaphore_wait(barrier, 5)
    loc_moves = []
    for q, (p_lon, p_mem, _) in enumerate(partners):
        move = pltpu.make_async_remote_copy(
            src_ref=loc_ref, dst_ref=loc_far.at[q],
            send_sem=loc_send.at[q], recv_sem=loc_recv.at[q],
            device_id=(p_mem, p_lon), device_id_type=MESH,
        )
        move.start()
        loc_moves.append(move)
    for step in (1, -1):
        signal(near_sem, along(step), lon)

    for c in range(CHUNKS // 2, CHUNKS):
        prepare_chunk(c)

    sub = lax.broadcasted_iota(jnp.int32, (TAIL, width), 0)
    row_i = lax.broadcasted_iota(jnp.int32, (half, half), 0)
    col_i = lax.broadcasted_iota(jnp.int32, (half, half), 1)

    def partial(picks, base, rank):
        for s in range(USE):
            u = picks(s)
            rel = u - base
            inside = jnp.logical_and(rel >= 0, rel < blocks)
            b = jnp.clip(rel, 0, blocks - 1)
            uf = jnp.full((1, width), u, jnp.int32).astype(F32)
            rf = jnp.full((1, width), rank, jnp.int32).astype(F32)
            t = (uf + 0.5) / blocks - 1.0 - (rf + 0.5) / ranks
            taper = jnp.exp(-0.5 * t * t) * jnp.full((1, width), inside.astype(jnp.int32), jnp.int32).astype(F32)
            block = pert[b]
            scaled = (block.astype(F32) * (weight[pl.ds(b, 1), :] * taper)).astype(BF16)
            high, low = halves(jnp.broadcast_to(innov[pl.ds(b, 1), :] * taper, (TAIL, width)))
            tail = jnp.where(sub == 0, high, jnp.where(sub == 1, low, 0.0)).astype(BF16)
            at = pl.ds(s * width, width)
            lhs[pl.ds(0, members), at] = scaled
            lhs[pl.ds(members, TAIL), at] = tail
            rhs[:, at] = block
        got = dot_nt(lhs[...], rhs[...])
        top, low = got[:half, :half], got[half:members, half:]
        packed = jnp.concatenate([jnp.where(row_i <= col_i, top, low), got[:half, half:]], axis=1)
        diag = jnp.concatenate(
            [jnp.sum(jnp.where(row_i == col_i, m, 0.0), axis=0, keepdims=True) for m in (top, low)], axis=1
        )
        return packed, got[members : members + 1] + got[members + 1 : members + 2], diag

    for j in range(PAT):
        rank = mem * PAT + j
        packed, force, diag = partial(lambda s: loc_ref[s, rank], blocks, rank)
        own[j] = packed
        own_tail[j, pl.ds(0, 1), :] = force
        own_tail[j, pl.ds(1, 1), :] = diag

    pl.semaphore_wait(near_sem, 2)
    for step in (2, -2):
        signal(far_sem, along(step), lon)

    row_id = lax.broadcasted_iota(jnp.int32, (TAIL, members), 0)
    part_moves = []
    for q, (p_lon, p_mem, s_q) in enumerate(partners):
        loc_moves[q].wait_recv()
        for j in range(PAT):
            rank = p_mem * PAT + j
            packed, force, diag = partial(lambda s: loc_far[q, s, rank], blocks - blocks * s_q, rank)
            send[q, j, pl.ds(0, half), :] = packed.astype(BF16)
            tail = jnp.zeros((TAIL, members), F32)
            for i, line in enumerate(halves(force) + halves(diag)):
                tail = jnp.where(row_id == i, line, tail)
            send[q, j, pl.ds(half, TAIL), :] = tail.astype(BF16)
            move = pltpu.make_async_remote_copy(
                src_ref=send.at[q, j], dst_ref=recv.at[q, j],
                send_sem=part_send.at[q, j], recv_sem=part_recv.at[q, j],
                device_id=(p_mem, p_lon), device_id_type=MESH,
            )
            move.start()
            part_moves.append(move)
        if q == 0:
            pl.semaphore_wait(far_sem, 2)
            signal(side_sem, crossed, lon)

    pl.semaphore_wait(side_sem, 1)
    order = []
    for step in (4, 3, -3, 2, -2, 1, -1, 0):
        column = (z + step + n_z) % n_z
        order.append(column * 2 + 1 - x)
        if step:
            order.append(column * 2 + x)
    state_moves = []
    for d, peer in enumerate(order):
        theirs = pl.ds(pl.multiple_of(peer * cols, cols), cols)
        move = pltpu.make_async_remote_copy(
            src_ref=state_ref.at[:, theirs], dst_ref=gathered.at[mine_rows, :],
            send_sem=in_send.at[d], recv_sem=in_recv.at[d],
            device_id=(peer, lon), device_id_type=MESH,
        )
        move.start()
        state_moves.append(move)

    eye = jnp.where(
        lax.broadcasted_iota(jnp.int32, (members, members), 0)
        == lax.broadcasted_iota(jnp.int32, (members, members), 1),
        1.0,
        0.0,
    )
    for move in part_moves:
        move.wait_recv()

    mats, roots, forces, scales = [], [], [], []
    for j in range(PAT):
        packed = own[j]
        force, diag = own_tail[j, pl.ds(0, 1), :], own_tail[j, pl.ds(1, 1), :]
        for q in range(2):
            packed = packed + recv[q, j, pl.ds(0, half), :].astype(F32)
            lines = recv[q, j, pl.ds(half, TAIL), :].astype(F32)
            force = force + lines[0:1] + lines[1:2]
            diag = diag + lines[2:3] + lines[3:4]
        diag = diag + (members - 1.0)
        mixed, cross = packed[:, :half], packed[:, half:]
        turned = mixed.T
        top = jnp.where(row_i == col_i, diag[:, :half], jnp.where(row_i < col_i, mixed, turned))
        low = jnp.where(row_i == col_i, diag[:, half:], jnp.where(row_i > col_i, mixed, turned))
        a = jnp.concatenate(
            [jnp.concatenate([top, cross], axis=1), jnp.concatenate([cross.T, low], axis=1)], axis=0
        )
        norm2 = jnp.sum(jnp.sum(a * a, axis=0, keepdims=True), axis=1, keepdims=True)
        inv = lax.rsqrt(norm2)
        mats.append(a * inv)
        scales.append(jnp.sqrt(inv))
        roots.append(None)
        forces.append(jnp.where(row_id == 0, jnp.broadcast_to(force, (TAIL, members)), 0.0))

    for step in range(ITERS):
        for j in range(PAT):
            e = mats[j]
            eb = e.astype(BF16)
            early = step < E_STEPS
            lead, gain = (1.5, -0.5) if early else (1.0, 0.5)
            forces[j] = lead * forces[j] + gain * dot(forces[j].astype(BF16), eb)
            if step == 0:
                roots[j] = lead * eye + gain * e
            else:
                roots[j] = lead * roots[j] + gain * dot(roots[j].astype(BF16), eb)
            if step < ITERS - 1:
                square = dot(eb, eb)
                cube = dot(square.astype(BF16), eb)
                if early:
                    e = 2.25 * e - 1.5 * square + 0.25 * cube
                    if step == E_STEPS - 1:
                        e = eye - e
                else:
                    e = 0.75 * square + 0.25 * cube
                mats[j] = e

    weights, rest = [], []
    for j in range(PAT):
        root = roots[j] * scales[j]
        mean_weight = dot((forces[j] * scales[j]).astype(BF16), root.astype(BF16))[0:1]
        w = jnp.sqrt(jnp.float32(members - 1.0)) * root + mean_weight
        high = w.astype(BF16)
        low = (w - high.astype(F32)).astype(BF16)
        weights.append((high, low))
        rest.append(1.0 - jnp.sum(w, axis=1, keepdims=True))

    keep.wait()
    for move in state_moves:
        move.wait_recv()
    ones = jnp.ones((TAIL, members), BF16)
    for j in range(PAT):
        at = pl.ds(j * pts, pts)
        points = gathered[:, at]
        high, low = weights[j]
        mean = dot(ones, points)[0:1] * (1.0 / members)
        answer[:, at] = (dot(high, points) + dot(low, points) + rest[j] * mean).astype(BF16)

    ans_moves = []
    for d, peer in enumerate(order):
        theirs = pl.ds(pl.multiple_of(peer * local, local), local)
        move = pltpu.make_async_remote_copy(
            src_ref=answer.at[theirs, :], dst_ref=out_ref.at[:, mine_cols],
            send_sem=ans_send.at[d], recv_sem=ans_recv.at[d],
            device_id=(peer, lon), device_id_type=MESH,
        )
        move.start()
        ans_moves.append(move)
    stay = pltpu.make_async_copy(answer.at[mine_rows, :], out_ref.at[:, mine_cols], here_sem.at[1])
    stay.start()
    for move in loc_moves + state_moves + part_moves:
        move.wait_send()
    stay.wait()
    for move in ans_moves:
        move.wait()


def solution(mesh):
    n_mem, n_lon = mesh.shape["mem"], mesh.shape["lon"]

    def body(state, hx, obs_value, obs_rinv, obs_count, loc_pattern):
        blocks, members, width = hx.shape
        local, points = state.shape
        cols = points // n_mem
        peers = n_mem - 1
        packed = members // 2 + TAIL
        dma, regular = pltpu.SemaphoreType.DMA, pltpu.SemaphoreType.REGULAR
        picks = loc_pattern.T
        args = (state, hx, obs_value, obs_rinv, obs_count, picks)
        return pl.pallas_call(
            functools.partial(kernel, n_mem, n_lon),
            out_shape=jax.ShapeDtypeStruct((local, points), BF16),
            in_specs=[pl.BlockSpec(memory_space=pl.ANY)] * len(args),
            out_specs=pl.BlockSpec(memory_space=pltpu.VMEM),
            scratch_shapes=[
                pltpu.VMEM((blocks, members, width), BF16),
                pltpu.VMEM((blocks, width), F32),
                pltpu.VMEM((blocks, width), F32),
                pltpu.SMEM((blocks,), jnp.int32),
                pltpu.SMEM(picks.shape, jnp.int32),
                pltpu.VMEM((blocks, width), F32),
                pltpu.VMEM((blocks, width), F32),
                pltpu.VMEM((members + TAIL, USE * width), BF16),
                pltpu.VMEM((members, USE * width), BF16),
                pltpu.VMEM((PAT, members // 2, members), F32),
                pltpu.VMEM((PAT, 8, members), F32),
                pltpu.VMEM((2, PAT, packed, members), BF16),
                pltpu.VMEM((2, PAT, packed, members), BF16),
                pltpu.VMEM((members, cols), BF16),
                pltpu.VMEM((members, cols), BF16),
                pltpu.SMEM((2,) + picks.shape, jnp.int32),
                dma((CHUNKS,)),
                dma((4,)),
                dma((2,)),
                dma((2,)),
                dma((2,)),
                dma((2, PAT)),
                dma((2, PAT)),
                dma((peers,)),
                dma((peers,)),
                dma((peers,)),
                dma((peers,)),
                regular,
                regular,
                regular,
            ],
            compiler_params=pltpu.CompilerParams(
                collective_id=0, has_side_effects=True, vmem_limit_bytes=LIMIT
            ),
        )(*args)

    in_specs = (
        P("mem", "lon"),
        P("lon", None, None),
        P("lon", None),
        P("lon", None),
        P("lon"),
        P("lon", None),
    )
    return jax.shard_map(body, mesh=mesh, in_specs=in_specs, out_specs=P("mem", "lon"), check_vma=False)


LIMIT = 63 << 20
```

```python
import functools

import jax
import jax.numpy as jnp
from jax import lax
from jax.experimental import pallas as pl
from jax.experimental.pallas import tpu as pltpu
from jax.sharding import PartitionSpec as P

MESH = pl.DeviceIdType.MESH
F32, BF16 = jnp.float32, jnp.bfloat16
USE = 8
PAT = 2
TAIL = 16
CHUNKS = 4
ITERS = 6
E_STEPS = 4


def dot(a, b):
    return lax.dot_general(a, b, (((1,), (0,)), ((), ())), preferred_element_type=F32)


def dot_nt(a, b):
    return lax.dot_general(a, b, (((1,), (1,)), ((), ())), preferred_element_type=F32)


def halves(x):
    high = x.astype(BF16).astype(F32)
    return high, x - high


def kernel(
    n_mem, n_lon,
    state_ref, hx_ref, value_hbm, rinv_hbm, count_hbm, loc_hbm,
    out_ref,
    pert, value_ref, rinv_ref, count_ref, loc_ref, weight, innov, lhs, rhs, own, own_tail, send, recv, gathered, answer, loc_far,
    hx_sem, small_sem, here_sem, loc_send, loc_recv, part_send, part_recv, in_send, in_recv, ans_send, ans_recv,
    near_sem, far_sem, side_sem,
):
    mem, lon = lax.axis_index("mem"), lax.axis_index("lon")
    blocks, members, width = hx_ref.shape
    half = members // 2
    local = state_ref.shape[0]
    cols = state_ref.shape[1] // n_mem
    pts = cols // PAT
    ranks = n_mem * PAT
    n_z = n_mem // 2
    z, x = mem // 2, mem % 2

    odd = lon % 2
    sign = 2 * odd - 1
    wrap = (lon + odd) % 8 == 0
    crossed = mem + 1 - 2 * x
    partners = (
        ((lon + sign + n_lon) % n_lon, jnp.where(wrap, crossed, mem), sign),
        ((lon - sign + n_lon) % n_lon, mem, -sign),
    )

    def along(step):
        return ((z + step + n_z) % n_z) * 2 + x

    def signal(sem, to_mem, to_lon):
        pl.semaphore_signal(sem, inc=1, device_id=(to_mem, to_lon), device_id_type=MESH)

    barrier = pltpu.get_barrier_semaphore()
    for p_lon, p_mem, _ in partners:
        signal(barrier, p_mem, p_lon)
    for step in (1, -1):
        signal(barrier, along(step), lon)
    signal(barrier, crossed, lon)

    smalls = []
    for i, (src, dst) in enumerate(
        ((loc_hbm, loc_ref), (count_hbm, count_ref), (rinv_hbm, rinv_ref), (value_hbm, value_ref))
    ):
        move = pltpu.make_async_copy(src, dst, small_sem.at[i])
        move.start()
        smalls.append(move)
    per = blocks // CHUNKS
    fetches = []
    for c in range(CHUNKS):
        part = pl.ds(c * per, per)
        fetch = pltpu.make_async_copy(hx_ref.at[part], pert.at[part], hx_sem.at[c])
        fetch.start()
        fetches.append(fetch)
    mine_rows = pl.ds(pl.multiple_of(mem * local, local), local)
    mine_cols = pl.ds(pl.multiple_of(mem * cols, cols), cols)
    keep = pltpu.make_async_copy(state_ref.at[:, mine_cols], gathered.at[mine_rows, :], here_sem.at[0])
    keep.start()
    for move in smalls:
        move.wait()

    lane = lax.broadcasted_iota(jnp.int32, (1, width), 1)

    def prepare(b):
        v = pert[b].astype(F32)
        mean = jnp.sum(v, axis=0, keepdims=True) * (1.0 / members)
        pert[b] = (v - mean).astype(BF16)
        w = jnp.where(lane < count_ref[b], rinv_ref[pl.ds(b, 1), :], 0.0)
        weight[pl.ds(b, 1), :] = w.astype(BF16).astype(F32)
        innov[pl.ds(b, 1), :] = (w * (value_ref[pl.ds(b, 1), :] - mean)).astype(BF16).astype(F32)

    def prepare_chunk(c):
        fetches[c].wait()

        @pl.loop(0, per // 4)
        def _(g):
            for k in range(4):
                prepare(c * per + g * 4 + k)

    for c in range(CHUNKS // 2):
        prepare_chunk(c)

    pl.semaphore_wait(barrier, 5)
    loc_moves = []
    for q, (p_lon, p_mem, _) in enumerate(partners):
        move = pltpu.make_async_remote_copy(
            src_ref=loc_ref, dst_ref=loc_far.at[q],
            send_sem=loc_send.at[q], recv_sem=loc_recv.at[q],
            device_id=(p_mem, p_lon), device_id_type=MESH,
        )
        move.start()
        loc_moves.append(move)
    for step in (1, -1):
        signal(near_sem, along(step), lon)

    for c in range(CHUNKS // 2, CHUNKS):
        prepare_chunk(c)

    sub = lax.broadcasted_iota(jnp.int32, (TAIL, width), 0)
    row_i = lax.broadcasted_iota(jnp.int32, (half, half), 0)
    col_i = lax.broadcasted_iota(jnp.int32, (half, half), 1)

    def partial(picks, base, rank):
        for s in range(USE):
            u = picks(s)
            rel = u - base
            inside = jnp.logical_and(rel >= 0, rel < blocks)
            b = jnp.clip(rel, 0, blocks - 1)
            uf = jnp.full((1, width), u, jnp.int32).astype(F32)
            rf = jnp.full((1, width), rank, jnp.int32).astype(F32)
            t = (uf + 0.5) / blocks - 1.0 - (rf + 0.5) / ranks
            taper = jnp.exp(-0.5 * t * t) * jnp.full((1, width), inside.astype(jnp.int32), jnp.int32).astype(F32)
            block = pert[b]
            scaled = (block.astype(F32) * (weight[pl.ds(b, 1), :] * taper)).astype(BF16)
            high, low = halves(jnp.broadcast_to(innov[pl.ds(b, 1), :] * taper, (TAIL, width)))
            tail = jnp.where(sub == 0, high, jnp.where(sub == 1, low, 0.0)).astype(BF16)
            at = pl.ds(s * width, width)
            lhs[pl.ds(0, members), at] = scaled
            lhs[pl.ds(members, TAIL), at] = tail
            rhs[:, at] = block
        got = dot_nt(lhs[...], rhs[...])
        top, low = got[:half, :half], got[half:members, half:]
        packed = jnp.concatenate([jnp.where(row_i <= col_i, top, low), got[:half, half:]], axis=1)
        diag = jnp.concatenate(
            [jnp.sum(jnp.where(row_i == col_i, m, 0.0), axis=0, keepdims=True) for m in (top, low)], axis=1
        )
        return packed, got[members : members + 1] + got[members + 1 : members + 2], diag

    for j in range(PAT):
        rank = mem * PAT + j
        packed, force, diag = partial(lambda s: loc_ref[s, rank], blocks, rank)
        own[j] = packed
        own_tail[j, pl.ds(0, 1), :] = force
        own_tail[j, pl.ds(1, 1), :] = diag

    pl.semaphore_wait(near_sem, 2)
    for step in (2, -2):
        signal(far_sem, along(step), lon)

    pl.semaphore_wait(far_sem, 2)
    signal(side_sem, crossed, lon)

    order = []
    for step in (4, 3, -3, 2, -2, 1, -1, 0):
        column = (z + step + n_z) % n_z
        order.append(column * 2 + 1 - x)
        if step:
            order.append(column * 2 + x)
    row_id = lax.broadcasted_iota(jnp.int32, (TAIL, members), 0)
    part_moves, state_moves = [], []
    for q, (p_lon, p_mem, s_q) in enumerate(partners):
        loc_moves[q].wait_recv()
        for j in range(PAT):
            rank = p_mem * PAT + j
            packed, force, diag = partial(lambda s: loc_far[q, s, rank], blocks - blocks * s_q, rank)
            send[q, j, pl.ds(0, half), :] = packed.astype(BF16)
            tail = jnp.zeros((TAIL, members), F32)
            for i, line in enumerate(halves(force) + halves(diag)):
                tail = jnp.where(row_id == i, line, tail)
            send[q, j, pl.ds(half, TAIL), :] = tail.astype(BF16)
            move = pltpu.make_async_remote_copy(
                src_ref=send.at[q, j], dst_ref=recv.at[q, j],
                send_sem=part_send.at[q, j], recv_sem=part_recv.at[q, j],
                device_id=(p_mem, p_lon), device_id_type=MESH,
            )
            move.start()
            part_moves.append(move)
        if q == 0:
            pl.semaphore_wait(side_sem, 1)
            for d, peer in enumerate(order):
                theirs = pl.ds(pl.multiple_of(peer * cols, cols), cols)
                move = pltpu.make_async_remote_copy(
                    src_ref=state_ref.at[:, theirs], dst_ref=gathered.at[mine_rows, :],
                    send_sem=in_send.at[d], recv_sem=in_recv.at[d],
                    device_id=(peer, lon), device_id_type=MESH,
                )
                move.start()
                state_moves.append(move)

    eye = jnp.where(
        lax.broadcasted_iota(jnp.int32, (members, members), 0)
        == lax.broadcasted_iota(jnp.int32, (members, members), 1),
        1.0,
        0.0,
    )
    for move in part_moves:
        move.wait_recv()

    mats, raws, roots, forces, scales = [], [], [], [], []
    for j in range(PAT):
        packed = own[j]
        force, diag = own_tail[j, pl.ds(0, 1), :], own_tail[j, pl.ds(1, 1), :]
        for q in range(2):
            packed = packed + recv[q, j, pl.ds(0, half), :].astype(F32)
            lines = recv[q, j, pl.ds(half, TAIL), :].astype(F32)
            force = force + lines[0:1] + lines[1:2]
            diag = diag + lines[2:3] + lines[3:4]
        diag = diag + (members - 1.0)
        mixed, cross = packed[:, :half], packed[:, half:]
        turned = mixed.T
        top = jnp.where(row_i == col_i, diag[:, :half], jnp.where(row_i < col_i, mixed, turned))
        low = jnp.where(row_i == col_i, diag[:, half:], jnp.where(row_i > col_i, mixed, turned))
        a = jnp.concatenate(
            [jnp.concatenate([top, cross], axis=1), jnp.concatenate([cross.T, low], axis=1)], axis=0
        )
        norm2 = jnp.sum(jnp.sum(a * a, axis=0, keepdims=True), axis=1, keepdims=True)
        inv = lax.rsqrt(norm2)
        mats.append(a * inv)
        raws.append((a.astype(BF16), inv))
        scales.append(jnp.sqrt(inv))
        roots.append(None)
        forces.append(force)

    def stacked(line):
        high, low = halves(line)
        return jnp.where(row_id == 0, high, jnp.where(row_id == 1, low, 0.0)).astype(BF16)

    def sum_rows(m):
        return m[0:1] + m[1:2]

    for step in range(ITERS):
        for j in range(PAT):
            e = mats[j]
            eb = e.astype(BF16)
            early = step < E_STEPS
            lead, gain = (1.5, -0.5) if early else (1.0, 0.5)
            forces[j] = lead * forces[j] + gain * sum_rows(dot(stacked(forces[j]), eb))
            if step == 0:
                roots[j] = lead * eye + gain * e
            else:
                roots[j] = lead * roots[j] + gain * dot(roots[j].astype(BF16), eb)
            if step < ITERS - 1:
                if step == 0:
                    raw, inv = raws[j]
                    square = dot(raw, raw) * (inv * inv)
                else:
                    square = dot(eb, eb)
                cube = dot(square.astype(BF16), eb)
                if early:
                    e = 2.25 * e - 1.5 * square + 0.25 * cube
                    if step == E_STEPS - 1:
                        e = eye - e
                else:
                    e = 0.75 * square + 0.25 * cube
                mats[j] = e

    weights, rest = [], []
    for j in range(PAT):
        root = roots[j] * scales[j]
        high, low = halves(root)
        u = stacked(forces[j] * scales[j])
        mean_weight = sum_rows(dot(u, high.astype(BF16)) + dot(u, low.astype(BF16)))
        w = jnp.sqrt(jnp.float32(members - 1.0)) * root + mean_weight
        high = w.astype(BF16)
        low = (w - high.astype(F32)).astype(BF16)
        weights.append((high, low))
        rest.append(1.0 - jnp.sum(w, axis=1, keepdims=True))

    keep.wait()
    for move in state_moves:
        move.wait_recv()
    ones = jnp.ones((TAIL, members), BF16)
    for j in range(PAT):
        at = pl.ds(j * pts, pts)
        points = gathered[:, at]
        high, low = weights[j]
        mean = dot(ones, points)[0:1] * (1.0 / members)
        answer[:, at] = (dot(high, points) + dot(low, points) + rest[j] * mean).astype(BF16)

    ans_moves = []
    for d, peer in enumerate(order):
        theirs = pl.ds(pl.multiple_of(peer * local, local), local)
        move = pltpu.make_async_remote_copy(
            src_ref=answer.at[theirs, :], dst_ref=out_ref.at[:, mine_cols],
            send_sem=ans_send.at[d], recv_sem=ans_recv.at[d],
            device_id=(peer, lon), device_id_type=MESH,
        )
        move.start()
        ans_moves.append(move)
    stay = pltpu.make_async_copy(answer.at[mine_rows, :], out_ref.at[:, mine_cols], here_sem.at[1])
    stay.start()
    for move in loc_moves + state_moves + part_moves:
        move.wait_send()
    stay.wait()
    for move in ans_moves:
        move.wait()


def solution(mesh):
    n_mem, n_lon = mesh.shape["mem"], mesh.shape["lon"]

    def body(state, hx, obs_value, obs_rinv, obs_count, loc_pattern):
        blocks, members, width = hx.shape
        local, points = state.shape
        cols = points // n_mem
        peers = n_mem - 1
        packed = members // 2 + TAIL
        dma, regular = pltpu.SemaphoreType.DMA, pltpu.SemaphoreType.REGULAR
        picks = loc_pattern.T
        args = (state, hx, obs_value, obs_rinv, obs_count, picks)
        return pl.pallas_call(
            functools.partial(kernel, n_mem, n_lon),
            out_shape=pltpu.VMEM((local, points), BF16),
            in_specs=[pl.BlockSpec(memory_space=pl.ANY)] * len(args),
            out_specs=pl.BlockSpec(memory_space=pltpu.VMEM),
            scratch_shapes=[
                pltpu.VMEM((blocks, members, width), BF16),
                pltpu.VMEM((blocks, width), F32),
                pltpu.VMEM((blocks, width), F32),
                pltpu.SMEM((blocks,), jnp.int32),
                pltpu.SMEM(picks.shape, jnp.int32),
                pltpu.VMEM((blocks, width), F32),
                pltpu.VMEM((blocks, width), F32),
                pltpu.VMEM((members + TAIL, USE * width), BF16),
                pltpu.VMEM((members, USE * width), BF16),
                pltpu.VMEM((PAT, members // 2, members), F32),
                pltpu.VMEM((PAT, 8, members), F32),
                pltpu.VMEM((2, PAT, packed, members), BF16),
                pltpu.VMEM((2, PAT, packed, members), BF16),
                pltpu.VMEM((members, cols), BF16),
                pltpu.VMEM((members, cols), BF16),
                pltpu.SMEM((2,) + picks.shape, jnp.int32),
                dma((CHUNKS,)),
                dma((4,)),
                dma((2,)),
                dma((2,)),
                dma((2,)),
                dma((2, PAT)),
                dma((2, PAT)),
                dma((peers,)),
                dma((peers,)),
                dma((peers,)),
                dma((peers,)),
                regular,
                regular,
                regular,
            ],
            compiler_params=pltpu.CompilerParams(
                collective_id=0, has_side_effects=True, vmem_limit_bytes=LIMIT
            ),
        )(*args)

    in_specs = (
        P("mem", "lon"),
        P("lon", None, None),
        P("lon", None),
        P("lon", None),
        P("lon"),
        P("lon", None),
    )
    return jax.shard_map(body, mesh=mesh, in_specs=in_specs, out_specs=P("mem", "lon"), check_vma=False)


LIMIT = 63 << 20
```

```python
import functools

import jax
import jax.numpy as jnp
from jax import lax
from jax.experimental import pallas as pl
from jax.experimental.pallas import tpu as pltpu
from jax.sharding import PartitionSpec as P

MESH = pl.DeviceIdType.MESH
F32, BF16 = jnp.float32, jnp.bfloat16
USE = 8
PAT = 2
TAIL = 16
CHUNKS = 4
ITERS = 6
E_STEPS = 4
AHEAD = 2


def dot(a, b):
    return lax.dot_general(a, b, (((1,), (0,)), ((), ())), preferred_element_type=F32)


def dot_nt(a, b):
    return lax.dot_general(a, b, (((1,), (1,)), ((), ())), preferred_element_type=F32)


def halves(x):
    high = x.astype(BF16).astype(F32)
    return high, x - high


def kernel(
    n_mem, n_lon,
    state_ref, hx_ref, value_hbm, rinv_hbm, count_hbm, loc_hbm,
    out_ref,
    pert, value_ref, rinv_ref, count_ref, loc_ref, weight, innov, own, own_tail, send, recv, gathered, answer, loc_far,
    hx_sem, small_sem, here_sem, loc_send, loc_recv, part_send, part_recv, in_send, in_recv, ans_send, ans_recv,
):
    mem, lon = lax.axis_index("mem"), lax.axis_index("lon")
    blocks, members, width = hx_ref.shape
    half = members // 2
    local = state_ref.shape[0]
    cols = state_ref.shape[1] // n_mem
    pts = cols // PAT
    ranks = n_mem * PAT
    n_z = n_mem // 2
    z, x = mem // 2, mem % 2

    odd = lon % 2
    sign = 2 * odd - 1
    wrap = (lon + odd) % 8 == 0
    crossed = mem + 1 - 2 * x
    partners = (
        ((lon + sign + n_lon) % n_lon, jnp.where(wrap, crossed, mem), sign),
        ((lon - sign + n_lon) % n_lon, mem, -sign),
    )

    def along(step):
        return ((z + step + n_z) % n_z) * 2 + x

    def signal(sem, to_mem, to_lon):
        pl.semaphore_signal(sem, inc=1, device_id=(to_mem, to_lon), device_id_type=MESH)

    barrier = pltpu.get_barrier_semaphore()
    for p_lon, p_mem, _ in partners:
        signal(barrier, p_mem, p_lon)
    order = []
    for step in (4, 3, -3, 2, -2, 1, -1, 0):
        column = (z + step + n_z) % n_z
        order.append(column * 2 + 1 - x)
        if step:
            order.append(column * 2 + x)
    for peer in order:
        signal(barrier, peer, lon)

    smalls = []
    for i, (src, dst) in enumerate(
        ((loc_hbm, loc_ref), (count_hbm, count_ref), (rinv_hbm, rinv_ref), (value_hbm, value_ref))
    ):
        move = pltpu.make_async_copy(src, dst, small_sem.at[i])
        move.start()
        smalls.append(move)
    per = blocks // CHUNKS
    fetches = []
    for c in range(CHUNKS):
        part = pl.ds(c * per, per)
        fetch = pltpu.make_async_copy(hx_ref.at[part], pert.at[part], hx_sem.at[c])
        fetch.start()
        fetches.append(fetch)
    mine_rows = pl.ds(pl.multiple_of(mem * local, local), local)
    mine_cols = pl.ds(pl.multiple_of(mem * cols, cols), cols)
    keep = pltpu.make_async_copy(state_ref.at[:, mine_cols], gathered.at[mine_rows, :], here_sem.at[0])
    keep.start()
    for move in smalls:
        move.wait()

    lane = lax.broadcasted_iota(jnp.int32, (1, width), 1)

    def prepare(b):
        v = pert[b].astype(F32)
        mean = jnp.sum(v, axis=0, keepdims=True) * (1.0 / members)
        pert[b] = (v - mean).astype(BF16)
        w = jnp.where(lane < count_ref[b], rinv_ref[pl.ds(b, 1), :], 0.0)
        weight[pl.ds(b, 1), :] = w.astype(BF16).astype(F32)
        innov[pl.ds(b, 1), :] = (w * (value_ref[pl.ds(b, 1), :] - mean)).astype(BF16).astype(F32)

    def prepare_chunk(c):
        fetches[c].wait()

        @pl.loop(0, per // 4)
        def _(g):
            for k in range(4):
                prepare(c * per + g * 4 + k)

    for c in range(CHUNKS // 2):
        prepare_chunk(c)

    pl.semaphore_wait(barrier, len(partners) + len(order))
    loc_moves = []
    for q, (p_lon, p_mem, _) in enumerate(partners):
        move = pltpu.make_async_remote_copy(
            src_ref=loc_ref, dst_ref=loc_far.at[q],
            send_sem=loc_send.at[q], recv_sem=loc_recv.at[q],
            device_id=(p_mem, p_lon), device_id_type=MESH,
        )
        move.start()
        loc_moves.append(move)
    state_moves = []
    for d, peer in enumerate(order):
        theirs = pl.ds(pl.multiple_of(peer * cols, cols), cols)
        move = pltpu.make_async_remote_copy(
            src_ref=state_ref.at[:, theirs], dst_ref=gathered.at[mine_rows, :],
            send_sem=in_send.at[d], recv_sem=in_recv.at[d],
            device_id=(peer, lon), device_id_type=MESH,
        )
        move.start()
        state_moves.append(move)

    for c in range(CHUNKS // 2, CHUNKS):
        prepare_chunk(c)

    sub = lax.broadcasted_iota(jnp.int32, (TAIL, width), 0)
    row_i = lax.broadcasted_iota(jnp.int32, (half, half), 0)
    col_i = lax.broadcasted_iota(jnp.int32, (half, half), 1)

    def partial(picks, base, rank):
        left, right = [], []
        for s in range(USE):
            u = picks(s)
            rel = u - base
            inside = jnp.logical_and(rel >= 0, rel < blocks)
            b = jnp.clip(rel, 0, blocks - 1)
            uf = jnp.full((1, width), u, jnp.int32).astype(F32)
            rf = jnp.full((1, width), rank, jnp.int32).astype(F32)
            t = (uf + 0.5) / blocks - 1.0 - (rf + 0.5) / ranks
            taper = jnp.exp(-0.5 * t * t) * jnp.full((1, width), inside.astype(jnp.int32), jnp.int32).astype(F32)
            block = pert[b]
            scaled = (block.astype(F32) * (weight[pl.ds(b, 1), :] * taper)).astype(BF16)
            high, low = halves(jnp.broadcast_to(innov[pl.ds(b, 1), :] * taper, (TAIL, width)))
            tail = jnp.where(sub == 0, high, jnp.where(sub == 1, low, 0.0)).astype(BF16)
            left.append(jnp.concatenate([scaled, tail], axis=0))
            right.append(block)
        got = dot_nt(jnp.concatenate(left, axis=1), jnp.concatenate(right, axis=1))
        top, low = got[:half, :half], got[half:members, half:]
        packed = jnp.concatenate([jnp.where(row_i <= col_i, top, low), got[:half, half:]], axis=1)
        diag = jnp.concatenate(
            [jnp.sum(jnp.where(row_i == col_i, m, 0.0), axis=0, keepdims=True) for m in (top, low)], axis=1
        )
        return packed, got[members : members + 1] + got[members + 1 : members + 2], diag

    for j in range(PAT):
        rank = mem * PAT + j
        packed, force, diag = partial(lambda s: loc_ref[s, rank], blocks, rank)
        own[j] = packed
        own_tail[j, pl.ds(0, 1), :] = force
        own_tail[j, pl.ds(1, 1), :] = diag

    row_id = lax.broadcasted_iota(jnp.int32, (TAIL, members), 0)
    part_moves = []
    for q, (p_lon, p_mem, s_q) in enumerate(partners):
        loc_moves[q].wait_recv()
        for j in range(PAT):
            rank = p_mem * PAT + j
            packed, force, diag = partial(lambda s: loc_far[q, s, rank], blocks - blocks * s_q, rank)
            send[q, j, pl.ds(0, half), :] = packed.astype(BF16)
            tail = jnp.zeros((TAIL, members), F32)
            for i, line in enumerate(halves(force) + halves(diag)):
                tail = jnp.where(row_id == i, line, tail)
            send[q, j, pl.ds(half, TAIL), :] = tail.astype(BF16)
            move = pltpu.make_async_remote_copy(
                src_ref=send.at[q, j], dst_ref=recv.at[q, j],
                send_sem=part_send.at[q, j], recv_sem=part_recv.at[q, j],
                device_id=(p_mem, p_lon), device_id_type=MESH,
            )
            move.start()
            part_moves.append(move)

    eye = jnp.where(
        lax.broadcasted_iota(jnp.int32, (members, members), 0)
        == lax.broadcasted_iota(jnp.int32, (members, members), 1),
        1.0,
        0.0,
    )
    for move in part_moves:
        move.wait_recv()

    mats, raws, forces, scales = [], [], [], []
    for j in range(PAT):
        packed = own[j]
        force, diag = own_tail[j, pl.ds(0, 1), :], own_tail[j, pl.ds(1, 1), :]
        for q in range(2):
            packed = packed + recv[q, j, pl.ds(0, half), :].astype(F32)
            lines = recv[q, j, pl.ds(half, TAIL), :].astype(F32)
            force = force + lines[0:1] + lines[1:2]
            diag = diag + lines[2:3] + lines[3:4]
        diag = diag + (members - 1.0)
        mixed, cross = packed[:, :half], packed[:, half:]
        turned = mixed.T
        top = jnp.where(row_i == col_i, diag[:, :half], jnp.where(row_i < col_i, mixed, turned))
        low = jnp.where(row_i == col_i, diag[:, half:], jnp.where(row_i > col_i, mixed, turned))
        a = jnp.concatenate(
            [jnp.concatenate([top, cross], axis=1), jnp.concatenate([cross.T, low], axis=1)], axis=0
        )
        norm2 = jnp.sum(jnp.sum(a * a, axis=0, keepdims=True), axis=1, keepdims=True)
        inv = lax.rsqrt(norm2)
        third = inv * (1.0 / 3.0)
        mats.append(a * third)
        raws.append((a.astype(BF16), third))
        scales.append(jnp.sqrt(inv) * 1.5**E_STEPS)
        forces.append(force)

    def stacked(line):
        high, low = halves(line)
        return jnp.where(row_id == 0, high, jnp.where(row_id == 1, low, 0.0)).astype(BF16)

    def sum_rows(m):
        return m[0:1] + m[1:2]

    loads, units = [], []
    for j in range(PAT):
        loads.append([raws[j][0]])
        units.append(raws[j][1])

    def raise_step(j, step):
        e, eb = mats[j], loads[j][step]
        square = dot(eb, eb)
        if step == 0:
            square = square * (units[j] * units[j])
        cube = dot(square.astype(BF16), eb)
        if step == 0:
            cube = cube * units[j]
        if step < E_STEPS:
            e = ((e - square) - square) + cube
            mats[j] = 2.25 * e if step < E_STEPS - 1 else 0.5 * eye - 3.375 * e
        else:
            mats[j] = 1.5 * square + cube
        loads[j].append(mats[j].astype(BF16))

    for step in range(AHEAD):
        for j in range(PAT):
            raise_step(j, step)

    keep.wait()
    for move in state_moves:
        move.wait_recv()
    points = gathered[...].astype(F32)
    state_mean = jnp.sum(points, axis=0, keepdims=True) * (1.0 / members)
    turned = (points - state_mean).T
    rows = [turned[j * pts : (j + 1) * pts] for j in range(PAT)]

    def apply_step(j, step):
        left = jnp.concatenate([rows[j].astype(BF16), stacked(forces[j])], axis=0)
        moved = dot(left, loads[j][step])
        if step == 0:
            moved = moved * units[j]
        force = sum_rows(moved[pts:])
        if step < E_STEPS:
            rows[j], forces[j] = rows[j] - moved[:pts], forces[j] - force
        else:
            rows[j], forces[j] = rows[j] + moved[:pts], forces[j] + force

    done = 0
    for step in range(AHEAD, ITERS):
        for j in range(PAT):
            if step < ITERS - 1:
                raise_step(j, step)
        upto = ITERS if step == ITERS - 1 else step + 1
        for k in range(done, upto):
            for j in range(PAT):
                apply_step(j, k)
        done = upto

    for j in range(PAT):
        s = scales[j]
        shift = jnp.sum(rows[j] * (forces[j] * (s * s)), axis=1, keepdims=True)
        y = (rows[j] * (s * jnp.sqrt(jnp.float32(members - 1.0))) + shift).T
        answer[:, pl.ds(j * pts, pts)] = (y + state_mean[:, j * pts : (j + 1) * pts]).astype(BF16)

    ans_moves = []
    for d, peer in enumerate(order):
        theirs = pl.ds(pl.multiple_of(peer * local, local), local)
        move = pltpu.make_async_remote_copy(
            src_ref=answer.at[theirs, :], dst_ref=out_ref.at[:, mine_cols],
            send_sem=ans_send.at[d], recv_sem=ans_recv.at[d],
            device_id=(peer, lon), device_id_type=MESH,
        )
        move.start()
        ans_moves.append(move)
    stay = pltpu.make_async_copy(answer.at[mine_rows, :], out_ref.at[:, mine_cols], here_sem.at[1])
    stay.start()
    for move in loc_moves + state_moves + part_moves:
        move.wait_send()
    stay.wait()
    for move in ans_moves:
        move.wait()


def solution(mesh):
    n_mem, n_lon = mesh.shape["mem"], mesh.shape["lon"]

    def body(state, hx, obs_value, obs_rinv, obs_count, loc_pattern):
        blocks, members, width = hx.shape
        local, points = state.shape
        cols = points // n_mem
        peers = n_mem - 1
        packed = members // 2 + TAIL
        dma = pltpu.SemaphoreType.DMA
        picks = loc_pattern.T
        args = (state, hx, obs_value, obs_rinv, obs_count, picks)
        return pl.pallas_call(
            functools.partial(kernel, n_mem, n_lon),
            out_shape=pltpu.VMEM((local, points), BF16),
            in_specs=[pl.BlockSpec(memory_space=pl.ANY)] * len(args),
            out_specs=pl.BlockSpec(memory_space=pltpu.VMEM),
            scratch_shapes=[
                pltpu.VMEM((blocks, members, width), BF16),
                pltpu.VMEM((blocks, width), F32),
                pltpu.VMEM((blocks, width), F32),
                pltpu.SMEM((blocks,), jnp.int32),
                pltpu.SMEM(picks.shape, jnp.int32),
                pltpu.VMEM((blocks, width), F32),
                pltpu.VMEM((blocks, width), F32),
                pltpu.VMEM((PAT, members // 2, members), F32),
                pltpu.VMEM((PAT, 8, members), F32),
                pltpu.VMEM((2, PAT, packed, members), BF16),
                pltpu.VMEM((2, PAT, packed, members), BF16),
                pltpu.VMEM((members, cols), BF16),
                pltpu.VMEM((members, cols), BF16),
                pltpu.SMEM((2,) + picks.shape, jnp.int32),
                dma((CHUNKS,)),
                dma((4,)),
                dma((2,)),
                dma((2,)),
                dma((2,)),
                dma((2, PAT)),
                dma((2, PAT)),
                dma((peers,)),
                dma((peers,)),
                dma((peers,)),
                dma((peers,)),
            ],
            compiler_params=pltpu.CompilerParams(
                collective_id=0, has_side_effects=True, vmem_limit_bytes=LIMIT
            ),
        )(*args)

    in_specs = (
        P("mem", "lon"),
        P("lon", None, None),
        P("lon", None),
        P("lon", None),
        P("lon"),
        P("lon", None),
    )
    return jax.shard_map(body, mesh=mesh, in_specs=in_specs, out_specs=P("mem", "lon"), check_vma=False)


LIMIT = 63 << 20
```

```python
import functools

import jax
import jax.numpy as jnp
from jax import lax
from jax.experimental import pallas as pl
from jax.experimental.pallas import tpu as pltpu
from jax.sharding import PartitionSpec as P

MESH = pl.DeviceIdType.MESH
F32, BF16 = jnp.float32, jnp.bfloat16
USE = 8
PAT = 2
TAIL = 16
CHUNKS = 4
ITERS = 6
E_STEPS = 4
AHEAD = 1


def dot(a, b):
    return lax.dot_general(a, b, (((1,), (0,)), ((), ())), preferred_element_type=F32)


def dot_nt(a, b):
    return lax.dot_general(a, b, (((1,), (1,)), ((), ())), preferred_element_type=F32)


def halves(x):
    high = x.astype(BF16).astype(F32)
    return high, x - high


def kernel(
    n_mem, n_lon,
    state_ref, hx_ref, value_hbm, rinv_hbm, count_hbm, loc_hbm,
    out_ref,
    pert, value_ref, rinv_ref, count_ref, loc_ref, weight, innov, own, own_tail, send, recv, gathered, answer, loc_far,
    hx_sem, small_sem, here_sem, loc_send, loc_recv, part_send, part_recv, in_send, in_recv, ans_send, ans_recv,
):
    mem, lon = lax.axis_index("mem"), lax.axis_index("lon")
    blocks, members, width = hx_ref.shape
    half = members // 2
    local = state_ref.shape[0]
    cols = state_ref.shape[1] // n_mem
    pts = cols // PAT
    ranks = n_mem * PAT
    n_z = n_mem // 2
    z, x = mem // 2, mem % 2

    odd = lon % 2
    sign = 2 * odd - 1
    wrap = (lon + odd) % 8 == 0
    crossed = mem + 1 - 2 * x
    partners = (
        ((lon + sign + n_lon) % n_lon, jnp.where(wrap, crossed, mem), sign),
        ((lon - sign + n_lon) % n_lon, mem, -sign),
    )

    def along(step):
        return ((z + step + n_z) % n_z) * 2 + x

    def signal(sem, to_mem, to_lon):
        pl.semaphore_signal(sem, inc=1, device_id=(to_mem, to_lon), device_id_type=MESH)

    barrier = pltpu.get_barrier_semaphore()
    for p_lon, p_mem, _ in partners:
        signal(barrier, p_mem, p_lon)
    order = []
    for step in (4, 3, -3, 2, -2, 1, -1, 0):
        column = (z + step + n_z) % n_z
        order.append(column * 2 + 1 - x)
        if step:
            order.append(column * 2 + x)
    for peer in order:
        signal(barrier, peer, lon)

    smalls = []
    for i, (src, dst) in enumerate(
        ((loc_hbm, loc_ref), (count_hbm, count_ref), (rinv_hbm, rinv_ref), (value_hbm, value_ref))
    ):
        move = pltpu.make_async_copy(src, dst, small_sem.at[i])
        move.start()
        smalls.append(move)
    per = blocks // CHUNKS
    fetches = []
    for c in range(CHUNKS):
        part = pl.ds(c * per, per)
        fetch = pltpu.make_async_copy(hx_ref.at[part], pert.at[part], hx_sem.at[c])
        fetch.start()
        fetches.append(fetch)
    mine_rows = pl.ds(pl.multiple_of(mem * local, local), local)
    mine_cols = pl.ds(pl.multiple_of(mem * cols, cols), cols)
    keep = pltpu.make_async_copy(state_ref.at[:, mine_cols], gathered.at[mine_rows, :], here_sem.at[0])
    keep.start()
    for move in smalls:
        move.wait()

    lane = lax.broadcasted_iota(jnp.int32, (1, width), 1)

    def prepare(b):
        v = pert[b].astype(F32)
        mean = jnp.sum(v, axis=0, keepdims=True) * (1.0 / members)
        pert[b] = (v - mean).astype(BF16)
        w = jnp.where(lane < count_ref[b], rinv_ref[pl.ds(b, 1), :], 0.0)
        weight[pl.ds(b, 1), :] = w.astype(BF16).astype(F32)
        innov[pl.ds(b, 1), :] = (w * (value_ref[pl.ds(b, 1), :] - mean)).astype(BF16).astype(F32)

    def prepare_chunk(c):
        fetches[c].wait()

        @pl.loop(0, per // 4)
        def _(g):
            for k in range(4):
                prepare(c * per + g * 4 + k)

    for c in range(CHUNKS // 2):
        prepare_chunk(c)

    pl.semaphore_wait(barrier, len(partners) + len(order))
    loc_moves = []
    for q, (p_lon, p_mem, _) in enumerate(partners):
        move = pltpu.make_async_remote_copy(
            src_ref=loc_ref, dst_ref=loc_far.at[q],
            send_sem=loc_send.at[q], recv_sem=loc_recv.at[q],
            device_id=(p_mem, p_lon), device_id_type=MESH,
        )
        move.start()
        loc_moves.append(move)
    state_moves = []
    for d, peer in enumerate(order):
        theirs = pl.ds(pl.multiple_of(peer * cols, cols), cols)
        move = pltpu.make_async_remote_copy(
            src_ref=state_ref.at[:, theirs], dst_ref=gathered.at[mine_rows, :],
            send_sem=in_send.at[d], recv_sem=in_recv.at[d],
            device_id=(peer, lon), device_id_type=MESH,
        )
        move.start()
        state_moves.append(move)

    for c in range(CHUNKS // 2, CHUNKS):
        prepare_chunk(c)

    sub = lax.broadcasted_iota(jnp.int32, (TAIL, width), 0)
    row_i = lax.broadcasted_iota(jnp.int32, (half, half), 0)
    col_i = lax.broadcasted_iota(jnp.int32, (half, half), 1)

    def partial(picks, base, rank):
        left, right = [], []
        for s in range(USE):
            u = picks(s)
            rel = u - base
            inside = jnp.logical_and(rel >= 0, rel < blocks)
            b = jnp.clip(rel, 0, blocks - 1)
            uf = jnp.full((1, width), u, jnp.int32).astype(F32)
            rf = jnp.full((1, width), rank, jnp.int32).astype(F32)
            t = (uf + 0.5) / blocks - 1.0 - (rf + 0.5) / ranks
            taper = jnp.exp(-0.5 * t * t) * jnp.full((1, width), inside.astype(jnp.int32), jnp.int32).astype(F32)
            block = pert[b]
            scaled = (block.astype(F32) * (weight[pl.ds(b, 1), :] * taper)).astype(BF16)
            high, low = halves(jnp.broadcast_to(innov[pl.ds(b, 1), :] * taper, (TAIL, width)))
            tail = jnp.where(sub == 0, high, jnp.where(sub == 1, low, 0.0)).astype(BF16)
            left.append(jnp.concatenate([scaled, tail], axis=0))
            right.append(block)
        got = dot_nt(jnp.concatenate(left, axis=1), jnp.concatenate(right, axis=1))
        top, low = got[:half, :half], got[half:members, half:]
        packed = jnp.concatenate([jnp.where(row_i <= col_i, top, low), got[:half, half:]], axis=1)
        diag = jnp.concatenate(
            [jnp.sum(jnp.where(row_i == col_i, m, 0.0), axis=0, keepdims=True) for m in (top, low)], axis=1
        )
        return packed, got[members : members + 1] + got[members + 1 : members + 2], diag

    for j in range(PAT):
        rank = mem * PAT + j
        packed, force, diag = partial(lambda s: loc_ref[s, rank], blocks, rank)
        own[j] = packed
        own_tail[j, pl.ds(0, 1), :] = force
        own_tail[j, pl.ds(1, 1), :] = diag

    row_id = lax.broadcasted_iota(jnp.int32, (TAIL, members), 0)
    part_moves = []
    for q, (p_lon, p_mem, s_q) in enumerate(partners):
        loc_moves[q].wait_recv()
        for j in range(PAT):
            rank = p_mem * PAT + j
            packed, force, diag = partial(lambda s: loc_far[q, s, rank], blocks - blocks * s_q, rank)
            send[q, j, pl.ds(0, half), :] = packed.astype(BF16)
            tail = jnp.zeros((TAIL, members), F32)
            for i, line in enumerate(halves(force) + halves(diag)):
                tail = jnp.where(row_id == i, line, tail)
            send[q, j, pl.ds(half, TAIL), :] = tail.astype(BF16)
            move = pltpu.make_async_remote_copy(
                src_ref=send.at[q, j], dst_ref=recv.at[q, j],
                send_sem=part_send.at[q, j], recv_sem=part_recv.at[q, j],
                device_id=(p_mem, p_lon), device_id_type=MESH,
            )
            move.start()
            part_moves.append(move)

    eye = jnp.where(
        lax.broadcasted_iota(jnp.int32, (members, members), 0)
        == lax.broadcasted_iota(jnp.int32, (members, members), 1),
        1.0,
        0.0,
    )
    keep.wait()
    for move in state_moves:
        move.wait_recv()
    points = gathered[...].astype(F32)
    state_mean = jnp.sum(points, axis=0, keepdims=True) * (1.0 / members)
    across = (points - state_mean).T
    rows = [across[j * pts : (j + 1) * pts] for j in range(PAT)]

    for move in part_moves:
        move.wait_recv()

    mats, raws, forces, scales = [], [], [], []
    for j in range(PAT):
        packed = own[j]
        force, diag = own_tail[j, pl.ds(0, 1), :], own_tail[j, pl.ds(1, 1), :]
        for q in range(2):
            packed = packed + recv[q, j, pl.ds(0, half), :].astype(F32)
            lines = recv[q, j, pl.ds(half, TAIL), :].astype(F32)
            force = force + lines[0:1] + lines[1:2]
            diag = diag + lines[2:3] + lines[3:4]
        diag = diag + (members - 1.0)
        mixed, cross = packed[:, :half], packed[:, half:]
        turned = mixed.T
        top = jnp.where(row_i == col_i, diag[:, :half], jnp.where(row_i < col_i, mixed, turned))
        low = jnp.where(row_i == col_i, diag[:, half:], jnp.where(row_i > col_i, mixed, turned))
        a = jnp.concatenate(
            [jnp.concatenate([top, cross], axis=1), jnp.concatenate([cross.T, low], axis=1)], axis=0
        )
        norm2 = jnp.sum(jnp.sum(a * a, axis=0, keepdims=True), axis=1, keepdims=True)
        inv = lax.rsqrt(norm2)
        third = inv * (1.0 / 3.0)
        mats.append(a * third)
        raws.append((a.astype(BF16), third))
        scales.append(jnp.sqrt(inv) * 1.5**E_STEPS)
        forces.append(force)

    def stacked(line):
        high, low = halves(line)
        return jnp.where(row_id == 0, high, jnp.where(row_id == 1, low, 0.0)).astype(BF16)

    def sum_rows(m):
        return m[0:1] + m[1:2]

    loads, units = [], []
    for j in range(PAT):
        loads.append([raws[j][0]])
        units.append(raws[j][1])

    def raise_step(j, step):
        e, eb = mats[j], loads[j][step]
        square = dot(eb, eb)
        if step == 0:
            square = square * (units[j] * units[j])
        cube = dot(square.astype(BF16), eb)
        if step == 0:
            cube = cube * units[j]
        if step < E_STEPS:
            e = ((e - square) - square) + cube
            mats[j] = 2.25 * e if step < E_STEPS - 1 else 0.5 * eye - 3.375 * e
        else:
            mats[j] = 1.5 * square + cube
        loads[j].append(mats[j].astype(BF16))

    def apply_step(j, step):
        left = jnp.concatenate([rows[j].astype(BF16), stacked(forces[j])], axis=0)
        moved = dot(left, loads[j][step])
        if step == 0:
            moved = moved * units[j]
        force = sum_rows(moved[pts:])
        if step < E_STEPS:
            rows[j], forces[j] = rows[j] - moved[:pts], forces[j] - force
        else:
            rows[j], forces[j] = rows[j] + moved[:pts], forces[j] + force

    for step in range(ITERS - 1 + AHEAD):
        for j in range(PAT):
            if step < ITERS - 1:
                raise_step(j, step)
        for j in range(PAT):
            if 0 <= step - AHEAD:
                apply_step(j, step - AHEAD)
    for j in range(PAT):
        apply_step(j, ITERS - 1)

    for j in range(PAT):
        s = scales[j]
        shift = jnp.sum(rows[j] * (forces[j] * (s * s)), axis=1, keepdims=True)
        y = (rows[j] * (s * jnp.sqrt(jnp.float32(members - 1.0))) + shift).T
        answer[:, pl.ds(j * pts, pts)] = (y + state_mean[:, j * pts : (j + 1) * pts]).astype(BF16)

    ans_moves = []
    for d, peer in enumerate(order):
        theirs = pl.ds(pl.multiple_of(peer * local, local), local)
        move = pltpu.make_async_remote_copy(
            src_ref=answer.at[theirs, :], dst_ref=out_ref.at[:, mine_cols],
            send_sem=ans_send.at[d], recv_sem=ans_recv.at[d],
            device_id=(peer, lon), device_id_type=MESH,
        )
        move.start()
        ans_moves.append(move)
    stay = pltpu.make_async_copy(answer.at[mine_rows, :], out_ref.at[:, mine_cols], here_sem.at[1])
    stay.start()
    for move in loc_moves + state_moves + part_moves:
        move.wait_send()
    stay.wait()
    for move in ans_moves:
        move.wait()


def solution(mesh):
    n_mem, n_lon = mesh.shape["mem"], mesh.shape["lon"]

    def body(state, hx, obs_value, obs_rinv, obs_count, loc_pattern):
        blocks, members, width = hx.shape
        local, points = state.shape
        cols = points // n_mem
        peers = n_mem - 1
        packed = members // 2 + TAIL
        dma = pltpu.SemaphoreType.DMA
        picks = loc_pattern.T
        args = (state, hx, obs_value, obs_rinv, obs_count, picks)
        return pl.pallas_call(
            functools.partial(kernel, n_mem, n_lon),
            out_shape=pltpu.VMEM((local, points), BF16),
            in_specs=[pl.BlockSpec(memory_space=pl.ANY)] * len(args),
            out_specs=pl.BlockSpec(memory_space=pltpu.VMEM),
            scratch_shapes=[
                pltpu.VMEM((blocks, members, width), BF16),
                pltpu.VMEM((blocks, width), F32),
                pltpu.VMEM((blocks, width), F32),
                pltpu.SMEM((blocks,), jnp.int32),
                pltpu.SMEM(picks.shape, jnp.int32),
                pltpu.VMEM((blocks, width), F32),
                pltpu.VMEM((blocks, width), F32),
                pltpu.VMEM((PAT, members // 2, members), F32),
                pltpu.VMEM((PAT, 8, members), F32),
                pltpu.VMEM((2, PAT, packed, members), BF16),
                pltpu.VMEM((2, PAT, packed, members), BF16),
                pltpu.VMEM((members, cols), BF16),
                pltpu.VMEM((members, cols), BF16),
                pltpu.SMEM((2,) + picks.shape, jnp.int32),
                dma((CHUNKS,)),
                dma((4,)),
                dma((2,)),
                dma((2,)),
                dma((2,)),
                dma((2, PAT)),
                dma((2, PAT)),
                dma((peers,)),
                dma((peers,)),
                dma((peers,)),
                dma((peers,)),
            ],
            compiler_params=pltpu.CompilerParams(
                collective_id=0, has_side_effects=True, vmem_limit_bytes=LIMIT
            ),
        )(*args)

    in_specs = (
        P("mem", "lon"),
        P("lon", None, None),
        P("lon", None),
        P("lon", None),
        P("lon"),
        P("lon", None),
    )
    return jax.shard_map(body, mesh=mesh, in_specs=in_specs, out_specs=P("mem", "lon"), check_vma=False)


LIMIT = 63 << 20
```

```python
import functools

import jax
import jax.numpy as jnp
from jax import lax
from jax.experimental import pallas as pl
from jax.experimental.pallas import tpu as pltpu
from jax.sharding import PartitionSpec as P

MESH = pl.DeviceIdType.MESH
F32, BF16 = jnp.float32, jnp.bfloat16
USE = 8
PAT = 2
TAIL = 16
CHUNKS = 4
ITERS = 6
E_STEPS = 4
AHEAD = 1


def dot(a, b):
    return lax.dot_general(a, b, (((1,), (0,)), ((), ())), preferred_element_type=F32)


def dot_nt(a, b):
    return lax.dot_general(a, b, (((1,), (1,)), ((), ())), preferred_element_type=F32)


def halves(x):
    high = x.astype(BF16).astype(F32)
    return high, x - high


def kernel(
    n_mem, n_lon,
    state_ref, hx_ref, value_hbm, rinv_hbm, count_hbm, loc_hbm,
    out_ref,
    pert, value_ref, rinv_ref, count_ref, loc_ref, weight, innov, own, own_tail, send, recv, gathered, answer, loc_far,
    hx_sem, small_sem, here_sem, loc_send, loc_recv, part_send, part_recv, in_send, in_recv, ans_send, ans_recv,
):
    mem, lon = lax.axis_index("mem"), lax.axis_index("lon")
    blocks, members, width = hx_ref.shape
    half = members // 2
    local = state_ref.shape[0]
    cols = state_ref.shape[1] // n_mem
    pts = cols // PAT
    ranks = n_mem * PAT
    n_z = n_mem // 2
    z, x = mem // 2, mem % 2

    odd = lon % 2
    sign = 2 * odd - 1
    wrap = (lon + odd) % 8 == 0
    crossed = mem + 1 - 2 * x
    partners = (
        ((lon + sign + n_lon) % n_lon, jnp.where(wrap, crossed, mem), sign),
        ((lon - sign + n_lon) % n_lon, mem, -sign),
    )

    def along(step):
        return ((z + step + n_z) % n_z) * 2 + x

    def signal(sem, to_mem, to_lon):
        pl.semaphore_signal(sem, inc=1, device_id=(to_mem, to_lon), device_id_type=MESH)

    barrier = pltpu.get_barrier_semaphore()
    for p_lon, p_mem, _ in partners:
        signal(barrier, p_mem, p_lon)
    order = []
    for step in (4, 3, -3, 2, -2, 1, -1, 0):
        column = (z + step + n_z) % n_z
        order.append(column * 2 + 1 - x)
        if step:
            order.append(column * 2 + x)

    smalls = []
    for i, (src, dst) in enumerate(
        ((loc_hbm, loc_ref), (count_hbm, count_ref), (rinv_hbm, rinv_ref), (value_hbm, value_ref))
    ):
        move = pltpu.make_async_copy(src, dst, small_sem.at[i])
        move.start()
        smalls.append(move)
    per = blocks // CHUNKS
    fetches = []
    for c in range(CHUNKS):
        part = pl.ds(c * per, per)
        fetch = pltpu.make_async_copy(hx_ref.at[part], pert.at[part], hx_sem.at[c])
        fetch.start()
        fetches.append(fetch)
    mine_rows = pl.ds(pl.multiple_of(mem * local, local), local)
    mine_cols = pl.ds(pl.multiple_of(mem * cols, cols), cols)
    keep = pltpu.make_async_copy(state_ref.at[:, mine_cols], gathered.at[mine_rows, :], here_sem.at[0])
    keep.start()
    for peer in order:
        signal(barrier, peer, lon)
    for move in smalls:
        move.wait()

    lane = lax.broadcasted_iota(jnp.int32, (1, width), 1)

    def prepare(b):
        v = pert[b].astype(F32)
        mean = jnp.sum(v, axis=0, keepdims=True) * (1.0 / members)
        pert[b] = (v - mean).astype(BF16)
        w = jnp.where(lane < count_ref[b], rinv_ref[pl.ds(b, 1), :], 0.0)
        weight[pl.ds(b, 1), :] = w.astype(BF16).astype(F32)
        innov[pl.ds(b, 1), :] = (w * (value_ref[pl.ds(b, 1), :] - mean)).astype(BF16).astype(F32)

    def prepare_chunk(c):
        fetches[c].wait()

        @pl.loop(0, per // 4)
        def _(g):
            for k in range(4):
                prepare(c * per + g * 4 + k)

    for c in range(CHUNKS // 2):
        prepare_chunk(c)

    pl.semaphore_wait(barrier, len(partners) + len(order))
    loc_moves = []
    for q, (p_lon, p_mem, _) in enumerate(partners):
        move = pltpu.make_async_remote_copy(
            src_ref=loc_ref, dst_ref=loc_far.at[q],
            send_sem=loc_send.at[q], recv_sem=loc_recv.at[q],
            device_id=(p_mem, p_lon), device_id_type=MESH,
        )
        move.start()
        loc_moves.append(move)
    state_moves = []
    for d, peer in enumerate(order):
        theirs = pl.ds(pl.multiple_of(peer * cols, cols), cols)
        move = pltpu.make_async_remote_copy(
            src_ref=state_ref.at[:, theirs], dst_ref=gathered.at[mine_rows, :],
            send_sem=in_send.at[d], recv_sem=in_recv.at[d],
            device_id=(peer, lon), device_id_type=MESH,
        )
        move.start()
        state_moves.append(move)

    for c in range(CHUNKS // 2, CHUNKS):
        prepare_chunk(c)

    sub = lax.broadcasted_iota(jnp.int32, (TAIL, width), 0)
    row_i = lax.broadcasted_iota(jnp.int32, (half, half), 0)
    col_i = lax.broadcasted_iota(jnp.int32, (half, half), 1)

    def partial(picks, base, rank):
        left, right = [], []
        for s in range(USE):
            u = picks(s)
            rel = u - base
            inside = jnp.logical_and(rel >= 0, rel < blocks)
            b = jnp.clip(rel, 0, blocks - 1)
            uf = jnp.full((1, width), u, jnp.int32).astype(F32)
            rf = jnp.full((1, width), rank, jnp.int32).astype(F32)
            t = (uf + 0.5) / blocks - 1.0 - (rf + 0.5) / ranks
            taper = jnp.exp(-0.5 * t * t) * jnp.full((1, width), inside.astype(jnp.int32), jnp.int32).astype(F32)
            block = pert[b]
            scaled = (block.astype(F32) * (weight[pl.ds(b, 1), :] * taper)).astype(BF16)
            high, low = halves(jnp.broadcast_to(innov[pl.ds(b, 1), :] * taper, (TAIL, width)))
            tail = jnp.where(sub == 0, high, jnp.where(sub == 1, low, 0.0)).astype(BF16)
            left.append(jnp.concatenate([scaled, tail], axis=0))
            right.append(block)
        got = dot_nt(jnp.concatenate(left, axis=1), jnp.concatenate(right, axis=1))
        top, low = got[:half, :half], got[half:members, half:]
        packed = jnp.concatenate([jnp.where(row_i <= col_i, top, low), got[:half, half:]], axis=1)
        diag = jnp.concatenate(
            [jnp.sum(jnp.where(row_i == col_i, m, 0.0), axis=0, keepdims=True) for m in (top, low)], axis=1
        )
        return packed, got[members : members + 1] + got[members + 1 : members + 2], diag

    for j in range(PAT):
        rank = mem * PAT + j
        packed, force, diag = partial(lambda s: loc_ref[s, rank], blocks, rank)
        own[j] = packed
        own_tail[j, pl.ds(0, 1), :] = force
        own_tail[j, pl.ds(1, 1), :] = diag

    row_id = lax.broadcasted_iota(jnp.int32, (TAIL, members), 0)
    part_moves = []
    for q, (p_lon, p_mem, s_q) in enumerate(partners):
        loc_moves[q].wait_recv()
        for j in range(PAT):
            rank = p_mem * PAT + j
            packed, force, diag = partial(lambda s: loc_far[q, s, rank], blocks - blocks * s_q, rank)
            send[q, j, pl.ds(0, half), :] = packed.astype(BF16)
            tail = jnp.zeros((TAIL, members), F32)
            for i, line in enumerate(halves(force) + halves(diag)):
                tail = jnp.where(row_id == i, line, tail)
            send[q, j, pl.ds(half, TAIL), :] = tail.astype(BF16)
            move = pltpu.make_async_remote_copy(
                src_ref=send.at[q, j], dst_ref=recv.at[q, j],
                send_sem=part_send.at[q, j], recv_sem=part_recv.at[q, j],
                device_id=(p_mem, p_lon), device_id_type=MESH,
            )
            move.start()
            part_moves.append(move)

    eye = jnp.where(
        lax.broadcasted_iota(jnp.int32, (members, members), 0)
        == lax.broadcasted_iota(jnp.int32, (members, members), 1),
        1.0,
        0.0,
    )
    keep.wait()
    for move in state_moves:
        move.wait_recv()
    points = gathered[...].astype(F32)
    state_mean = jnp.sum(points, axis=0, keepdims=True) * (1.0 / members)
    across = (points - state_mean).T
    rows = [across[j * pts : (j + 1) * pts] for j in range(PAT)]

    for move in part_moves:
        move.wait_recv()

    mats, raws, forces, scales = [], [], [], []
    for j in range(PAT):
        packed = own[j]
        force, diag = own_tail[j, pl.ds(0, 1), :], own_tail[j, pl.ds(1, 1), :]
        for q in range(2):
            packed = packed + recv[q, j, pl.ds(0, half), :].astype(F32)
            lines = recv[q, j, pl.ds(half, TAIL), :].astype(F32)
            force = force + lines[0:1] + lines[1:2]
            diag = diag + lines[2:3] + lines[3:4]
        diag = diag + (members - 1.0)
        mixed, cross = packed[:, :half], packed[:, half:]
        turned = mixed.T
        top = jnp.where(row_i == col_i, diag[:, :half], jnp.where(row_i < col_i, mixed, turned))
        low = jnp.where(row_i == col_i, diag[:, half:], jnp.where(row_i > col_i, mixed, turned))
        a = jnp.concatenate(
            [jnp.concatenate([top, cross], axis=1), jnp.concatenate([cross.T, low], axis=1)], axis=0
        )
        norm2 = jnp.sum(jnp.sum(a * a, axis=0, keepdims=True), axis=1, keepdims=True)
        inv = lax.rsqrt(norm2)
        third = inv * (1.0 / 3.0)
        mats.append(a * third)
        raws.append((a.astype(BF16), third))
        scales.append(jnp.sqrt(inv) * 1.5**E_STEPS)
        forces.append(force)

    def stacked(line):
        high, low = halves(line)
        return jnp.where(row_id == 0, high, jnp.where(row_id == 1, low, 0.0)).astype(BF16)

    def sum_rows(m):
        return m[0:1] + m[1:2]

    loads, units = [], []
    for j in range(PAT):
        loads.append([raws[j][0]])
        units.append(raws[j][1])

    def raise_step(j, step):
        e, eb = mats[j], loads[j][step]
        square = dot(eb, eb)
        if step == 0:
            square = square * (units[j] * units[j])
        cube = dot(square.astype(BF16), eb)
        if step == 0:
            cube = cube * units[j]
        if step < E_STEPS:
            e = ((e - square) - square) + cube
            mats[j] = 2.25 * e if step < E_STEPS - 1 else 0.5 * eye - 3.375 * e
        else:
            mats[j] = 1.5 * square + cube
        loads[j].append(mats[j].astype(BF16))

    def apply_step(j, step):
        left = jnp.concatenate([rows[j].astype(BF16), stacked(forces[j])], axis=0)
        moved = dot(left, loads[j][step])
        if step == 0:
            moved = moved * units[j]
        force = sum_rows(moved[pts:])
        if step < E_STEPS:
            rows[j], forces[j] = rows[j] - moved[:pts], forces[j] - force
        else:
            rows[j], forces[j] = rows[j] + moved[:pts], forces[j] + force

    for step in range(ITERS - 1 + AHEAD):
        for j in range(PAT):
            if step < ITERS - 1:
                raise_step(j, step)
        for j in range(PAT):
            if 0 <= step - AHEAD:
                apply_step(j, step - AHEAD)
    for j in range(PAT):
        apply_step(j, ITERS - 1)

    for j in range(PAT):
        s = scales[j]
        shift = jnp.sum(rows[j] * (forces[j] * (s * s)), axis=1, keepdims=True)
        y = (rows[j] * (s * jnp.sqrt(jnp.float32(members - 1.0))) + shift).T
        answer[:, pl.ds(j * pts, pts)] = (y + state_mean[:, j * pts : (j + 1) * pts]).astype(BF16)

    ans_moves = []
    for d, peer in enumerate(order):
        theirs = pl.ds(pl.multiple_of(peer * local, local), local)
        move = pltpu.make_async_remote_copy(
            src_ref=answer.at[theirs, :], dst_ref=out_ref.at[:, mine_cols],
            send_sem=ans_send.at[d], recv_sem=ans_recv.at[d],
            device_id=(peer, lon), device_id_type=MESH,
        )
        move.start()
        ans_moves.append(move)
    stay = pltpu.make_async_copy(answer.at[mine_rows, :], out_ref.at[:, mine_cols], here_sem.at[1])
    stay.start()
    for move in loc_moves + state_moves + part_moves:
        move.wait_send()
    stay.wait()
    for move in ans_moves:
        move.wait()


def solution(mesh):
    n_mem, n_lon = mesh.shape["mem"], mesh.shape["lon"]

    def body(state, hx, obs_value, obs_rinv, obs_count, loc_pattern):
        blocks, members, width = hx.shape
        local, points = state.shape
        cols = points // n_mem
        peers = n_mem - 1
        packed = members // 2 + TAIL
        dma = pltpu.SemaphoreType.DMA
        picks = loc_pattern.T
        args = (state, hx, obs_value, obs_rinv, obs_count, picks)
        return pl.pallas_call(
            functools.partial(kernel, n_mem, n_lon),
            out_shape=pltpu.VMEM((local, points), BF16),
            in_specs=[pl.BlockSpec(memory_space=pl.ANY)] * len(args),
            out_specs=pl.BlockSpec(memory_space=pltpu.VMEM),
            scratch_shapes=[
                pltpu.VMEM((blocks, members, width), BF16),
                pltpu.VMEM((blocks, width), F32),
                pltpu.VMEM((blocks, width), F32),
                pltpu.SMEM((blocks,), jnp.int32),
                pltpu.SMEM(picks.shape, jnp.int32),
                pltpu.VMEM((blocks, width), F32),
                pltpu.VMEM((blocks, width), F32),
                pltpu.VMEM((PAT, members // 2, members), F32),
                pltpu.VMEM((PAT, 8, members), F32),
                pltpu.VMEM((2, PAT, packed, members), BF16),
                pltpu.VMEM((2, PAT, packed, members), BF16),
                pltpu.VMEM((members, cols), BF16),
                pltpu.VMEM((members, cols), BF16),
                pltpu.SMEM((2,) + picks.shape, jnp.int32),
                dma((CHUNKS,)),
                dma((4,)),
                dma((2,)),
                dma((2,)),
                dma((2,)),
                dma((2, PAT)),
                dma((2, PAT)),
                dma((peers,)),
                dma((peers,)),
                dma((peers,)),
                dma((peers,)),
            ],
            compiler_params=pltpu.CompilerParams(
                collective_id=0, has_side_effects=True, vmem_limit_bytes=LIMIT
            ),
        )(*args)

    in_specs = (
        P("mem", "lon"),
        P("lon", None, None),
        P("lon", None),
        P("lon", None),
        P("lon"),
        P("lon", None),
    )
    return jax.shard_map(body, mesh=mesh, in_specs=in_specs, out_specs=P("mem", "lon"), check_vma=False)


LIMIT = 63 << 20
```
